512 devices in a mesh: row: 16 (over x_lo, y), col: 32 (over x_hi, z, core).
Axes of the slice: x: 4 (x_hi: 2, x_lo: 2; x = x_hi * 2 + x_lo), y: 8, z: 8, core: 2. Of those that a mesh axis runs over, the one named last changes fastest.
Arguments:
- tokens: bfloat16 [2048, 6144], P('row', 'col'), may hold values from -6 to 6
- w_query: bfloat16 [6144, 4096], P('row', 'col'), may hold values from -0.078125 to 0.078125
- w_key: bfloat16 [6144, 4096], P('row', 'col'), may hold values from -0.078125 to 0.078125
- w_value: bfloat16 [6144, 4096], P('row', 'col'), may hold values from -0.078125 to 0.078125
- w_out: bfloat16 [4096, 6144], P('row', 'col'), may hold values from -0.09375 to 0.09375
- key_cache: bfloat16 [32768, 4096], P('row', 'col'), may hold values from -6 to 6
- value_cache: bfloat16 [32768, 4096], P('row', 'col'), may hold values from -6 to 6
- query_gain: float32 [128], replicated, may hold values from 1 to 2.5
- key_gain: float32 [128], replicated, may hold values from 1 to 2.5
- out_gate: float32 [6144], P('col'), may hold values from 0.5 to 2
- cotangent: bfloat16 [2048, 6144], P('row', 'col'), may hold values from -6 to 6
Outputs:
- layer_out: bfloat16 [2048, 6144], P('row', 'col')
- attention_cotangent: bfloat16 [2048, 4096], P('row', 'col')
The draws below stay inside these ranges and needn't reach their ends.
All inputs are finite; a program needn't handle non-finite values.
Results may differ from the reference program's by a relative error of at most 0.012.
Values may be sent and summed in bfloat16 or wider, within the bound.
A program may use at most 64 MiB of HBM per device.

```python
import math
import jax
import jax.numpy as jnp
from jax import lax

D = 6144
HEAD_DIM = 128
HEADS = 32
FA = 4096
TOKENS = 2048
CACHE = 32768


def levels(stream_key, dims, shards, smallest, high):
    loudness = 1.0
    for dim, shards_of in shards:
        heights = jax.random.uniform(jax.random.fold_in(jax.random.fold_in(stream_key, 6), dim), (shards_of,), jnp.float32, smallest / len(shards), high / len(shards))
        loudness = loudness * jnp.repeat(jnp.exp(heights), dims[dim] // shards_of).reshape((-1,) + (1,) * (len(dims) - 1 - dim))
    return loudness


def bell_draw(rng, dims, spread, limit, cuts=(), held_as=jnp.bfloat16):
    array = spread * jax.random.normal(rng, dims, jnp.float32)
    if cuts:
        array = array * levels(rng, dims, cuts, -0.22, 0.18)
    return jnp.clip(array, -limit, limit).astype(held_as)


def setup_inputs(seed: int = 0) -> dict:
    key_of = jax.random.split(jax.random.key(seed), 12)
    return {
        "tokens": bell_draw(key_of[0], (TOKENS, D), 1.0, 6.0, ((0, 16), (1, 32))),
        "w_query": bell_draw(key_of[1], (D, FA), D ** -0.5, 0.078125, ((0, 16), (1, 32))),
        "w_key": bell_draw(key_of[2], (D, FA), D ** -0.5, 0.078125, ((0, 16), (1, 32))),
        "w_value": bell_draw(key_of[3], (D, FA), D ** -0.5, 0.078125, ((0, 16), (1, 32))),
        "w_out": bell_draw(key_of[4], (FA, D), FA ** -0.5, 0.09375, ((0, 16), (1, 32))),
        "key_cache": bell_draw(key_of[5], (CACHE, FA), 1.0, 6.0, ((0, 16), (1, 32))),
        "value_cache": bell_draw(key_of[6], (CACHE, FA), 1.0, 6.0, ((0, 16), (1, 32))),
        "query_gain": jnp.clip(jnp.exp(jax.random.uniform(key_of[7], (HEAD_DIM,), jnp.float32, math.log(1.0), math.log(2.5))), 1.0, 2.5),
        "key_gain": jnp.clip(jnp.exp(jax.random.uniform(key_of[8], (HEAD_DIM,), jnp.float32, math.log(1.0), math.log(2.5))), 1.0, 2.5),
        "out_gate": jnp.clip(jnp.exp(math.log(2.0) - 1.3862944 * jax.random.uniform(key_of[9], (D,), jnp.float32) ** levels(key_of[9], (D,), ((0, 32),), -0.2, 0.2)), 0.5, 2.0),
        "cotangent": bell_draw(key_of[10], (TOKENS, D), 1.0, 6.0, ((0, 16), (1, 32))),
    }


epsilon = 1e-06

def norm_heads(values, gain):
    wide = values.astype(jnp.float32)
    mean_square = lax.optimization_barrier(jnp.mean(wide * wide, axis=-1, keepdims=True))
    return (wide * lax.rsqrt(mean_square + epsilon) * gain.astype(jnp.float32)).astype(jnp.bfloat16)

def reference(tokens, w_query, w_key, w_value, w_out, key_cache, value_cache, query_gain, key_gain, out_gate, cotangent):
    query = jnp.dot(tokens, w_query, preferred_element_type=jnp.float32).astype(jnp.bfloat16)
    key_new = jnp.dot(tokens, w_key, preferred_element_type=jnp.float32).astype(jnp.bfloat16)
    value_new = jnp.dot(tokens, w_value, preferred_element_type=jnp.float32).astype(jnp.bfloat16)
    slab_rows = query.shape[0]
    query_norm = norm_heads(query.reshape(slab_rows, HEADS, HEAD_DIM), query_gain)
    key_all = jnp.concatenate([key_cache, key_new], axis=0)
    key_norm = norm_heads(key_all.reshape(-1, HEADS, HEAD_DIM), key_gain)
    value_all = jnp.concatenate([value_cache, value_new], axis=0).reshape(-1, HEADS, HEAD_DIM)
    scale = HEAD_DIM ** (-0.5)

    def one_head(operands):
        query_head, key_head, value_head = operands
        scores = jnp.dot(query_head.astype(jnp.float32), key_head.astype(jnp.float32).T) * scale
        weights = jnp.exp(scores)
        totals = lax.optimization_barrier(jnp.sum(weights, axis=1, keepdims=True))
        weights_low = lax.optimization_barrier(weights.astype(jnp.bfloat16))
        numerators = jnp.dot(weights_low.astype(jnp.float32), value_head.astype(jnp.float32))
        return (numerators / totals).astype(jnp.bfloat16)
    per_head = lax.map(one_head, (query_norm.transpose(1, 0, 2), key_norm.transpose(1, 0, 2), value_all.transpose(1, 0, 2)))
    attention = per_head.transpose(1, 0, 2).reshape(slab_rows, HEADS * HEAD_DIM)
    branch = jnp.dot(attention, w_out, preferred_element_type=jnp.float32)
    layer_out = (tokens.astype(jnp.float32) + out_gate.astype(jnp.float32) * branch).astype(jnp.bfloat16)
    scaled = (cotangent.astype(jnp.float32) * out_gate.astype(jnp.float32)).astype(jnp.bfloat16)
    attention_cotangent = jnp.dot(scaled, w_out.T, preferred_element_type=jnp.float32).astype(jnp.bfloat16)
    return (layer_out, attention_cotangent)
```

```python
import functools
import math

import jax
import jax.numpy as jnp
from jax import lax
from jax.experimental import pallas as pl
from jax.experimental.pallas import tpu as pltpu
from jax.sharding import PartitionSpec as P

MESH = pl.DeviceIdType.MESH
epsilon = 1e-06
f32 = jnp.float32
bf16 = jnp.bfloat16
LAST = (((1,), (1,)), ((), ()))


def norm_rows(values, gain):
    wide = values.astype(f32)
    mean_square = jnp.mean(wide * wide, axis=-1, keepdims=True)
    return (wide * lax.rsqrt(mean_square + epsilon) * gain).astype(bf16)


def ring_order(n):
    order = [0]
    for d in range(1, n // 2 + 1):
        order.append(d)
        if (n - d) % n != d:
            order.append(n - d)
    return order


def kernel(
    n,
    tokens,
    w_query,
    w_key,
    w_value,
    w_out,
    key_cache,
    value_cache,
    query_gain,
    key_gain,
    out_gate,
    cotangent,
    layer_out,
    grad_out,
    tok,
    wall,
    wout,
    keys,
    vals,
    scaled,
    qsend,
    qpart,
    kvsend,
    kvpart,
    queries,
    acc,
    nsend,
    nrecv,
    gsend,
    grecv,
    att,
    s_t,
    r_t,
    s_w,
    r_w,
    s_wo,
    r_wo,
    s_wx,
    r_wx,
    s_g,
    r_g,
    s_q,
    r_q,
    s_kv,
    r_kv,
    s_qa,
    r_qa,
    s_n,
    r_n,
    s_gr,
    r_gr,
    s_a,
    r_a,
):
    rows, dcols = tokens.shape
    head = query_gain.shape[1]
    cached = key_cache.shape[0]
    row = lax.axis_index("row")
    col = lax.axis_index("col")
    xl, y = row // n, row % n
    xh, z, k = col // (2 * n), (col // 2) % n, col % 2

    def dev(xl_, y_, xh_, z_, k_):
        return (xl_ * n + y_, (xh_ * n + z_) * 2 + k_)

    order = ring_order(n)
    slot_of = {d: i for i, d in enumerate(order)}

    def dist(d):
        return min(d, n - d)

    row_rel = sorted([(a, b) for b in order for a in (0, 1)], key=lambda t: dist(t[1]) + t[0])
    row_inv = [row_rel.index((a, (n - b) % n)) for a, b in row_rel]
    col_rel = [
        (a, b, c)
        for b in order
        for a in (0, 1)
        for c in (0, 1)
        if (a, b, c) != (0, 0, 0)
    ]
    col_inv = [col_rel.index((a, (n - b) % n, c)) for a, b, c in col_rel]

    def row_peer(a, b):
        return dev((xl + a) % 2, (y + b) % n, xh, z, k)

    def col_peer(a, b, c):
        return dev(xl, y, (xh + a) % 2, (z + b) % n, (k + c) % 2)

    def remote(src, dst, ssem, rsem, to):
        return pltpu.make_async_remote_copy(
            src_ref=src, dst_ref=dst, send_sem=ssem, recv_sem=rsem, device_id=to, device_id_type=MESH
        )

    any_peer = col_peer(0, 0, 1)

    def arrived(dst, ssem, rsem):
        remote(dst, dst, ssem, rsem, any_peer).wait_recv()

    sends = []

    def send(src, dst, ssem, rsem, to):
        copy = remote(src, dst, ssem, rsem, to)
        copy.start()
        sends.append(copy)

    barrier = pltpu.get_barrier_semaphore()
    off_diagonal = y != z
    twin = dev(xl, z, xh, y, k)

    @pl.when(off_diagonal)
    def _():
        pl.semaphore_signal(barrier, inc=1, device_id=twin, device_id_type=MESH)

    for a, b in row_rel[1:]:
        pl.semaphore_signal(barrier, inc=1, device_id=row_peer(a, b), device_id_type=MESH)
    for rel in col_rel:
        pl.semaphore_signal(barrier, inc=1, device_id=col_peer(*rel), device_id_type=MESH)

    kgain = key_gain[...]
    keys[0:cached, :] = norm_rows(key_cache[...], kgain)
    vals[0:cached, 0:head] = value_cache[...]
    vals[:, head:] = jnp.ones((vals.shape[0], vals.shape[1] - head), bf16)
    scaled[...] = (cotangent[...].astype(f32) * out_gate[...]).astype(bf16)

    peers = len(row_rel) - 1 + len(col_rel)

    @pl.when(off_diagonal)
    def _():
        pl.semaphore_wait(barrier, peers + 1)

    @pl.when(jnp.logical_not(off_diagonal))
    def _():
        pl.semaphore_wait(barrier, peers)

    first = tok.at[0, 0, 0]
    transpose = remote(tokens, first, s_t, r_t, twin)
    stay = pltpu.make_async_copy(tokens, first, r_t)

    @pl.when(off_diagonal)
    def _():
        transpose.start()

    @pl.when(jnp.logical_not(off_diagonal))
    def _():
        stay.start()

    x_near = row_peer(1, 0)
    for i, w in enumerate((w_query, w_key, w_value)):
        send(w, wall.at[xl, :, pl.ds(i * head, head)], s_w.at[i], r_w.at[i], x_near)
        wall[xl, :, i * head : (i + 1) * head] = w[...]

    for d in order[1:]:
        send(w_out, wout.at[row], s_wo.at[slot_of[d]], r_wo.at[slot_of[(n - d) % n]], row_peer(0, d))
    wout[row] = w_out[...]
    send(w_out, wout.at[row], s_wx.at[0], r_wx.at[0], x_near)

    @pl.when(off_diagonal)
    def _():
        transpose.wait_recv()

    @pl.when(jnp.logical_not(off_diagonal))
    def _():
        stay.wait()

    def gather_start(buf, ss, rs):
        for d in reversed(order[1:]):
            i = slot_of[d]
            j = slot_of[(n - d) % n]
            send(buf.at[0, 0, 0], buf.at[0, 0, j], ss.at[0, i], rs.at[0, j], col_peer(0, d, 0))

    def gather_z(buf, ss, rs, i):
        if i:
            arrived(buf.at[0, 0, i], ss.at[0, i], rs.at[0, i])
        send(buf.at[0, 0, i], buf.at[1, 0, i], ss.at[1, i], rs.at[1, i], col_peer(1, 0, 0))
        send(buf.at[0, 0, i], buf.at[0, 1, i], ss.at[2, i], rs.at[2, i], col_peer(0, 0, 1))

    def gather_x(buf, ss, rs, i):
        arrived(buf.at[1, 0, i], ss.at[1, i], rs.at[1, i])
        send(buf.at[1, 0, i], buf.at[1, 1, i], ss.at[3, i], rs.at[3, i], col_peer(0, 0, 1))

    def gather_core(buf, ss, rs, i):
        arrived(buf.at[0, 1, i], ss.at[2, i], rs.at[2, i])
        arrived(buf.at[1, 1, i], ss.at[3, i], rs.at[3, i])

    def project(slots, lo, width):
        total = None
        lines = rows * len(slots)
        for a in (0, 1):
            for c in (0, 1):
                left = tok[a, c, slots[0] : slots[0] + len(slots)].reshape(lines, dcols)
                start = pl.multiple_of(((k + c) % 2) * dcols, 16)
                right = wall[(xh + a) % 2, pl.ds(start, dcols), lo : lo + width]
                term = jnp.dot(left, right, preferred_element_type=f32)
                total = term if total is None else total + term
        return total.astype(bf16)

    gather_start(tok, s_g, r_g)
    half = max(n // 2, 1)
    conditional = []

    def ship(i, src, dst, ssem, rsem):
        owner = (z + order[i]) % n
        copy = remote(src, dst, ssem, rsem, dev(xl, owner, xh, z, k))

        @pl.when(owner != y)
        def _():
            copy.start()

        conditional.append((owner != y, copy))

    def keep(i, dst, value):
        owner = (z + order[i]) % n

        @pl.when(owner == y)
        def _():
            dst[y] = value

    weights_here = False
    for step in range(n + 2):
        if step < n:
            gather_z(tok, s_g, r_g, step)
        if 1 <= step <= n:
            gather_x(tok, s_g, r_g, step - 1)
        if step >= 2:
            i = step - 2
            gather_core(tok, s_g, r_g, i)
            if not weights_here:
                weights_here = True
                for j in range(3):
                    part = wall.at[1 - xl, :, pl.ds(j * head, head)]
                    arrived(part, s_w.at[j], r_w.at[j])
            if (i + 1) % half == 0:
                slots = list(range(i + 1 - half, i + 1))
                product = project(slots, 0, head)
                for m, s in enumerate(slots):
                    value = product[m * rows : (m + 1) * rows]
                    qsend[s] = value
                    keep(s, qpart, value)
                    ship(s, qsend.at[s], qpart.at[y], s_q.at[s], r_q.at[y])

    for h in range(n // half):
        slots = list(range(h * half, (h + 1) * half))
        product = project(slots, head, 2 * head)
        for m, s in enumerate(slots):
            value = product[m * rows : (m + 1) * rows]
            kvsend[s] = value
            keep(s, kvpart, value)

    for i in range(1, n):
        src = (y + order[i]) % n
        arrived(wout.at[xl * n + src], s_wo.at[i], r_wo.at[i])
        send(wout.at[xl * n + src], wout.at[xl * n + src], s_wx.at[i], r_wx.at[i], x_near)

    for i in range(1, n):
        src = (y + i) % n
        arrived(qpart.at[src], s_q.at[0], r_q.at[src])
    query = qpart[0].astype(f32)
    for i in range(1, n):
        query = query + qpart[i].astype(f32)
    queries[0] = norm_rows(query.astype(bf16), query_gain[...])
    for i in range(1, 2 * n):
        j = row_inv[i]
        send(queries.at[0], queries.at[j], s_qa.at[i], r_qa.at[j], row_peer(*row_rel[i]))
    for s in range(n):
        ship(s, kvsend.at[s], kvpart.at[y], s_kv.at[s], r_kv.at[y])

    for i in range(n):
        src = (y + order[i]) % n
        arrived(wout.at[(1 - xl) * n + src], s_wx.at[i], r_wx.at[i])

    def grad_block(j, _):
        terms = lax.dot_general(scaled[...], wout[j], LAST, preferred_element_type=f32)
        for c in (0, 1):
            gsend[2 * j + c] = terms[:, c * head : (c + 1) * head].astype(bf16)
        return 0

    lax.fori_loop(0, 2 * n, grad_block, 0)
    for i, (a, b, c) in enumerate(col_rel):
        j = col_inv[i]
        _, target = col_peer(a, b, c)
        send(gsend.at[target], grecv.at[j], s_gr.at[i], r_gr.at[j], col_peer(a, b, c))

    factor = math.log2(math.e) * head ** (-0.5)
    group = max(n // 2, 1)
    n_groups = 2 * n // group
    lines = group * rows
    chunk = min(512, cached)

    def attend(g, lo, size):
        query = queries[g * group : (g + 1) * group].reshape(lines, head)
        scores = lax.dot_general(query, keys[pl.ds(lo, size), :], LAST, preferred_element_type=f32)
        weights = jnp.exp2(scores * factor).astype(bf16)
        return jnp.dot(weights, vals[pl.ds(lo, size), :], preferred_element_type=f32)

    def attend_cached(g):
        for i in range(max(g * group, 1), (g + 1) * group):
            arrived(queries.at[i], s_qa.at[i], r_qa.at[i])
        acc[g] = attend(g, 0, chunk)

        def step(i, _):
            acc[g] += attend(g, pl.multiple_of(i * chunk, chunk), chunk)
            return 0

        lax.fori_loop(1, cached // chunk, step, 0)

    same = lax.broadcasted_iota(jnp.int32, (rows, rows), 0) == lax.broadcasted_iota(
        jnp.int32, (rows, rows), 1
    )

    def attend_new(g):
        acc[g] += attend(g, cached, rows)
        for m in range(group):
            i = g * group + m
            block = acc[g, m * rows : (m + 1) * rows, :]
            total = jnp.sum(jnp.where(same, block[:, head:], 0.0), axis=0, keepdims=True)
            high = total.astype(bf16)
            low = (total - high.astype(f32)).astype(bf16)
            where = nsend.at[i] if i else nrecv.at[0]
            where[0:rows, :] = block[:, :head].astype(bf16)
            line = lax.broadcasted_iota(jnp.int32, (16, rows), 0)
            tail = jnp.where(
                line == 0,
                jnp.broadcast_to(high.astype(f32), (16, rows)),
                jnp.where(line == 1, jnp.broadcast_to(low.astype(f32), (16, rows)), 0.0),
            )
            where[rows:, :] = tail.astype(bf16)
            if i:
                j = row_inv[i]
                send(nsend.at[i], nrecv.at[j], s_n.at[i], r_n.at[j], row_peer(*row_rel[i]))

    early = n_groups // 2
    for g in range(early):
        attend_cached(g)
    for i in range(1, n):
        src = (y + i) % n
        arrived(kvpart.at[src], s_kv.at[0], r_kv.at[src])
    fresh = kvpart[0].astype(f32)
    for i in range(1, n):
        fresh = fresh + kvpart[i].astype(f32)
    fresh = fresh.astype(bf16)
    keys[cached:, :] = norm_rows(fresh[:, :head], kgain)
    vals[cached:, 0:head] = fresh[:, head:]
    for g in range(early):
        attend_new(g)
    for g in range(early, n_groups):
        attend_cached(g)
        attend_new(g)

    _, mine = col_peer(0, 0, 0)
    grad = gsend[mine].astype(f32)
    for j in range(len(col_rel)):
        arrived(grecv.at[j], s_gr.at[j], r_gr.at[j])
        grad = grad + grecv[j].astype(f32)
    grad_out[...] = grad.astype(bf16)

    for j in range(1, 2 * n):
        arrived(nrecv.at[j], s_n.at[j], r_n.at[j])
    summed = nrecv[0].astype(f32)
    for j in range(1, 2 * n):
        summed = summed + nrecv[j].astype(f32)
    total = summed[rows : rows + 1, :] + summed[rows + 1 : rows + 2, :]
    total = jnp.sum(jnp.where(same, jnp.broadcast_to(total, (rows, rows)), 0.0), axis=1, keepdims=True)
    att[0, 0, 0] = (summed[0:rows, :] / total).astype(bf16)

    gather_start(att, s_a, r_a)
    branch = jnp.zeros((rows, dcols), f32)
    for step in range(n + 2):
        if step < n:
            gather_z(att, s_a, r_a, step)
        if 1 <= step <= n:
            gather_x(att, s_a, r_a, step - 1)
        if step >= 2:
            i = step - 2
            gather_core(att, s_a, r_a, i)
            for a in (0, 1):
                chip = ((xh + a) % 2) * n + (z + order[i]) % n
                for c in (0, 1):
                    start = pl.multiple_of(((k + c) % 2) * head, 16)
                    right = wout[chip, pl.ds(start, head), :]
                    branch = branch + jnp.dot(att[a, c, i], right, preferred_element_type=f32)
    layer_out[...] = (tokens[...].astype(f32) + out_gate[...] * branch).astype(bf16)

    @pl.when(off_diagonal)
    def _():
        transpose.wait_send()

    for copy in sends:
        copy.wait_send()
    for away, copy in conditional:

        @pl.when(away)
        def _(copy=copy):
            copy.wait_send()


def body(n, *args):
    tokens, w_query, w_key, w_value, w_out, key_cache, value_cache, query_gain, key_gain, out_gate, cotangent = args
    rows, dcols = tokens.shape
    head = query_gain.shape[0]
    kin = w_query.shape[0]
    cached = key_cache.shape[0]
    group = max(n // 2, 1)
    vmem = pl.BlockSpec(memory_space=pltpu.VMEM)
    dma = pltpu.SemaphoreType.DMA
    col_peers = 4 * n - 1
    scratch = [
        pltpu.VMEM((2, 2, n, rows, dcols), bf16),
        pltpu.VMEM((2, kin, 3 * head), bf16),
        pltpu.VMEM((2 * n,) + w_out.shape, bf16),
        pltpu.VMEM((cached + rows, head), bf16),
        pltpu.VMEM((cached + rows, 2 * head), bf16),
        pltpu.VMEM((rows, dcols), bf16),
        pltpu.VMEM((n, rows, head), bf16),
        pltpu.VMEM((n, rows, head), bf16),
        pltpu.VMEM((n, rows, 2 * head), bf16),
        pltpu.VMEM((n, rows, 2 * head), bf16),
        pltpu.VMEM((2 * n, rows, head), bf16),
        pltpu.VMEM((2 * n // group, group * rows, 2 * head), f32),
        pltpu.VMEM((2 * n, rows + 16, head), bf16),
        pltpu.VMEM((2 * n, rows + 16, head), bf16),
        pltpu.VMEM((4 * n, rows, head), bf16),
        pltpu.VMEM((col_peers, rows, head), bf16),
        pltpu.VMEM((2, 2, n, rows, head), bf16),
        dma,
        dma,
        dma((3,)),
        dma((3,)),
        dma((n,)),
        dma((n,)),
        dma((n,)),
        dma((n,)),
        dma((4, n)),
        dma((4, n)),
        dma((n,)),
        dma((n,)),
        dma((n,)),
        dma((n,)),
        dma((2 * n,)),
        dma((2 * n,)),
        dma((2 * n,)),
        dma((2 * n,)),
        dma((col_peers,)),
        dma((col_peers,)),
        dma((4, n)),
        dma((4, n)),
    ]
    return pl.pallas_call(
        functools.partial(kernel, n),
        name="attention_block",
        out_shape=(
            jax.ShapeDtypeStruct((rows, dcols), bf16),
            jax.ShapeDtypeStruct((rows, head), bf16),
        ),
        in_specs=[vmem] * 11,
        out_specs=(vmem, vmem),
        scratch_shapes=scratch,
        compiler_params=pltpu.CompilerParams(
            collective_id=0, has_side_effects=True, vmem_limit_bytes=60 * 1024 * 1024
        ),
    )(
        tokens,
        w_query,
        w_key,
        w_value,
        w_out,
        key_cache,
        value_cache,
        query_gain.reshape(1, head),
        key_gain.reshape(1, head),
        out_gate.reshape(1, dcols),
        cotangent,
    )


def solution(mesh):
    n = mesh.shape["row"] // 2
    both = P("row", "col")
    placed = (both,) * 7 + (P(), P(), P("col"), both)
    return jax.shard_map(
        functools.partial(body, n),
        mesh=mesh,
        in_specs=placed,
        out_specs=(both, both),
        check_vma=False,
    )
```

```python
import functools
import math

import jax
import jax.numpy as jnp
from jax import lax
from jax.experimental import pallas as pl
from jax.experimental.pallas import tpu as pltpu
from jax.sharding import PartitionSpec as P

MESH = pl.DeviceIdType.MESH
epsilon = 1e-06
f32 = jnp.float32
bf16 = jnp.bfloat16
FIRST = (((0,), (0,)), ((), ()))
LAST = (((1,), (1,)), ((), ()))


def norm_rows(values, gain):
    wide = values.astype(f32)
    mean_square = jnp.mean(wide * wide, axis=-1, keepdims=True)
    return (wide * lax.rsqrt(mean_square + epsilon) * gain).astype(bf16)


def ring_order(n):
    order = [0]
    for d in range(1, n // 2 + 1):
        order.append(d)
        if (n - d) % n != d:
            order.append(n - d)
    return order


def kernel(
    n,
    tokens,
    w_query,
    w_key,
    w_value,
    w_out,
    key_cache,
    value_cache,
    query_gain,
    key_gain,
    out_gate,
    cotangent,
    layer_out,
    grad_out,
    tok,
    wall,
    wout,
    keys,
    vals,
    scaled,
    qsend,
    qpart,
    kvsend,
    kvpart,
    queries,
    acc,
    nsend,
    nrecv,
    gsend,
    gpair,
    gsum,
    grecv,
    att,
    kraw,
    tokv,
    cotv,
    s_in,
    s_t,
    r_t,
    s_w,
    r_w,
    s_wo,
    r_wo,
    s_wx,
    r_wx,
    s_g,
    r_g,
    s_q,
    r_q,
    s_kv,
    r_kv,
    s_qa,
    r_qa,
    s_n,
    r_n,
    s_gp,
    r_gp,
    s_gr,
    r_gr,
    s_a,
    r_a,
):
    dcols, rows = tokens.shape
    head = query_gain.shape[1]
    cached = key_cache.shape[0]
    row = lax.axis_index("row")
    col = lax.axis_index("col")
    xl, y = row // n, row % n
    xh, z, k = col // (2 * n), (col // 2) % n, col % 2

    def dev(xl_, y_, xh_, z_, k_):
        return (xl_ * n + y_, (xh_ * n + z_) * 2 + k_)

    order = ring_order(n)
    slot_of = {d: i for i, d in enumerate(order)}

    group = max(n // 2, 1)
    near, far = order[:group], order[group:]
    row_rel = [(0, b) for b in near + far] + [(1, b) for b in near + far]
    row_inv = [row_rel.index((a, (n - b) % n)) for a, b in row_rel]
    own = row_rel.index((0, 0))
    others = [i for i in range(2 * n) if i != own]
    if n == 8:
        hops = {0: ((2, None), (6, None), (1, None), (7, None))}
        hops[2] = ((7, None), (6, 0))
        hops[6] = ((1, None), (2, 1))
        turns = [slot_of[d] for d in (0, 2, 6, 1, 7, 3, 5, 4)]
    else:
        hops = {0: tuple((d, None) for d in range(1, n))}
        turns = list(range(n))
    chip_rel = [(a, b) for b in order for a in (0, 1)]
    chip_inv = [chip_rel.index((a, (n - b) % n)) for a, b in chip_rel]
    col_rel = [
        (a, b, c)
        for b in order
        for a in (0, 1)
        for c in (0, 1)
        if (a, b, c) != (0, 0, 0)
    ]

    def row_peer(a, b):
        return dev((xl + a) % 2, (y + b) % n, xh, z, k)

    def col_peer(a, b, c):
        return dev(xl, y, (xh + a) % 2, (z + b) % n, (k + c) % 2)

    def remote(src, dst, ssem, rsem, to):
        return pltpu.make_async_remote_copy(
            src_ref=src, dst_ref=dst, send_sem=ssem, recv_sem=rsem, device_id=to, device_id_type=MESH
        )

    any_peer = col_peer(0, 0, 1)

    def arrived(dst, ssem, rsem):
        remote(dst, dst, ssem, rsem, any_peer).wait_recv()

    sends = []

    def send(src, dst, ssem, rsem, to):
        copy = remote(src, dst, ssem, rsem, to)
        copy.start()
        sends.append(copy)

    barrier = pltpu.get_barrier_semaphore()
    off_diagonal = y != z
    twin = dev(xl, z, xh, y, k)

    @pl.when(off_diagonal)
    def _():
        pl.semaphore_signal(barrier, inc=1, device_id=twin, device_id_type=MESH)

    for i in others:
        pl.semaphore_signal(barrier, inc=1, device_id=row_peer(*row_rel[i]), device_id_type=MESH)
    for rel in col_rel:
        pl.semaphore_signal(barrier, inc=1, device_id=col_peer(*rel), device_id_type=MESH)

    local = [
        (key_cache, kraw),
        (cotangent, cotv),
        (value_cache, vals.at[pl.ds(0, cached), pl.ds(0, head)]),
        (w_query, wall.at[xl, :, pl.ds(0, head)]),
        (w_key, wall.at[xl, :, pl.ds(head, head)]),
        (w_value, wall.at[xl, :, pl.ds(2 * head, head)]),
        (w_out, wout.at[row]),
        (tokens, tokv),
    ]
    loads = [pltpu.make_async_copy(src, dst, s_in.at[i]) for i, (src, dst) in enumerate(local)]
    for load in loads:
        load.start()
    vals[:, head:] = jnp.ones((vals.shape[0], vals.shape[1] - head), bf16)
    kgain = key_gain[...]
    gate = jnp.transpose(jnp.broadcast_to(out_gate[...], (rows, dcols)))
    loads[0].wait()
    keys[0:cached, :] = norm_rows(kraw[...], kgain)
    loads[1].wait()
    scaled[...] = jnp.transpose((cotv[...].astype(f32) * gate).astype(bf16))
    for load in loads[2:]:
        load.wait()

    peers = len(row_rel) - 1 + len(col_rel)

    @pl.when(off_diagonal)
    def _():
        pl.semaphore_wait(barrier, peers + 1)

    @pl.when(jnp.logical_not(off_diagonal))
    def _():
        pl.semaphore_wait(barrier, peers)

    first = tok.at[0, 2 * xh + k]
    transpose = remote(tokens, first, s_t, r_t, twin)
    stay = pltpu.make_async_copy(tokens, first, r_t)

    @pl.when(off_diagonal)
    def _():
        transpose.start()

    @pl.when(jnp.logical_not(off_diagonal))
    def _():
        stay.start()

    x_near = row_peer(1, 0)
    for i, w in enumerate((w_query, w_key, w_value)):
        send(w, wall.at[xl, :, pl.ds(i * head, head)], s_w.at[i], r_w.at[i], x_near)


    def pass_weights(*slots):
        for i in slots:
            if i < n:
                block = wout.at[xl * n + (y + order[i]) % n]
                arrived(block, s_wo.at[i], r_wo.at[i])
                send(block, block, s_wx.at[i], r_wx.at[i], x_near)

    @pl.when(off_diagonal)
    def _():
        transpose.wait_recv()

    @pl.when(jnp.logical_not(off_diagonal))
    def _():
        stay.wait()

    def place(a, c):
        return ((xh + a) % 2) * 2 + (k + c) % 2

    def relay(buf, ss, rs, a, d):
        block = buf.at[slot_of[d], place(a, 0)]
        for step, only in hops.get(d, ()):
            if only is None or only == a:
                j = slot_of[(d - step) % n]
                send(block, buf.at[j, place(a, 0)], ss.at[a, j], rs.at[a, j], col_peer(0, step, 0))

    def share(buf, ss, rs, a, i):
        block = buf.at[i, place(a, 0)]
        send(block, block, ss.at[2 + a, i], rs.at[2 + a, i], col_peer(0, 0, 1))

    def gather_start(buf, ss, rs):
        block = buf.at[0, place(0, 0)]
        send(block, block, ss.at[1, 0], rs.at[1, 0], col_peer(1, 0, 0))
        relay(buf, ss, rs, 0, 0)
        share(buf, ss, rs, 0, 0)

    def gather_other(buf, ss, rs):
        arrived(buf.at[0, place(1, 0)], ss.at[1, 0], rs.at[1, 0])
        relay(buf, ss, rs, 1, 0)
        share(buf, ss, rs, 1, 0)

    def gather_z(buf, ss, rs, i):
        if i:
            for a in (0, 1):
                arrived(buf.at[i, place(a, 0)], ss.at[a, i], rs.at[a, i])
                relay(buf, ss, rs, a, order[i])
                share(buf, ss, rs, a, i)

    def gather_core(buf, ss, rs, i):
        for a in (0, 1):
            arrived(buf.at[i, place(a, 1)], ss.at[2 + a, i], rs.at[2 + a, i])

    lag = 2

    def project(slot, lo, width):
        left = tok[slot].reshape(4 * dcols, rows)
        right = wall[:, :, lo : lo + width].reshape(4 * dcols, width)
        return lax.dot_general(left, right, FIRST, preferred_element_type=f32).astype(bf16)

    gather_start(tok, s_g, r_g)
    for d in order[1:]:
        send(w_out, wout.at[row], s_wo.at[slot_of[d]], r_wo.at[slot_of[(n - d) % n]], row_peer(0, d))
    gather_other(tok, s_g, r_g)
    send(w_out, wout.at[row], s_wx.at[0], r_wx.at[0], x_near)
    weights_here = False
    for step in range(n + lag):
        if step < n:
            gather_z(tok, s_g, r_g, turns[step])
        if step >= lag:
            i = turns[step - lag]
            gather_core(tok, s_g, r_g, i)
            if not weights_here:
                weights_here = True
                for j in range(3):
                    part = wall.at[1 - xl, :, pl.ds(j * head, head)]
                    arrived(part, s_w.at[j], r_w.at[j])
            value = project(i, 0, 3 * head)
            owner = (z + order[i]) % n
            qsend[owner] = value[:, :head]
            kvsend[owner] = value[:, head:]
    for d in reversed(order[1:]):
        owner = (y + d) % n
        send(qsend.at[owner], qpart.at[y], s_q.at[d], r_q.at[y], row_peer(0, d))
    qpart[y] = qsend[y]
    kvpart[y] = kvsend[y]
    pass_weights(*range(1, n))

    for i in range(1, n):
        src = (y + i) % n
        arrived(qpart.at[src], s_q.at[0], r_q.at[src])
    query = qpart[0].astype(f32)
    for i in range(1, n):
        query = query + qpart[i].astype(f32)
    queries[own] = norm_rows(query.astype(bf16), query_gain[...])
    send(queries.at[own], queries.at[n], s_qa.at[n], r_qa.at[n], x_near)
    for d in order[1:]:
        i = slot_of[d]
        j = slot_of[n - d]
        send(queries.at[own], queries.at[j], s_qa.at[i], r_qa.at[j], row_peer(0, d))
    for d in reversed(order[1:]):
        owner = (y + d) % n
        send(kvsend.at[owner], kvpart.at[y], s_kv.at[d], r_kv.at[y], row_peer(0, d))

    def grad_block(j, _):
        terms = jnp.dot(scaled[...], wout[j], preferred_element_type=f32)
        for c in (0, 1):
            gsend[c, j] = terms[:, c * head : (c + 1) * head].astype(bf16)
        return 0

    def grad_terms():
        for i in range(n):
            src = (y + order[i]) % n
            arrived(wout.at[(1 - xl) * n + src], s_wx.at[i], r_wx.at[i])

        lax.fori_loop(0, 2 * n, grad_block, 0)
        send(gsend.at[1 - k], gpair, s_gp, r_gp, col_peer(0, 0, 1))

    def grad_send():
        arrived(gpair, s_gp, r_gp)
        gsum[...] = (gsend[k].astype(f32) + gpair[...].astype(f32)).astype(bf16)
        for i, (a, b) in enumerate(chip_rel):
            if i:
                chip = ((xh + a) % 2) * n + (z + b) % n
                j = chip_inv[i]
                send(gsum.at[chip], grecv.at[j], s_gr.at[i], r_gr.at[j], col_peer(a, b, 0))

    factor = math.log2(math.e) * head ** (-0.5)
    n_groups = 2 * n // group
    lines = group * rows
    chunk = min(512, cached)

    def attend(g, lo, size):
        query = queries[g * group : (g + 1) * group].reshape(lines, head)
        scores = lax.dot_general(query, keys[pl.ds(lo, size), :], LAST, preferred_element_type=f32)
        weights = jnp.exp2(scores * factor).astype(bf16)
        return jnp.dot(weights, vals[pl.ds(lo, size), :], preferred_element_type=f32)

    def attend_cached(g):
        for i in range(g * group, (g + 1) * group):
            if i == own:
                continue
            arrived(queries.at[i], s_qa.at[i], r_qa.at[i])
            if i < n:
                send(queries.at[i], queries.at[n + i], s_qa.at[n + i], r_qa.at[n + i], x_near)
        acc[g] = attend(g, 0, chunk)

        def step(i, _):
            acc[g] += attend(g, pl.multiple_of(i * chunk, chunk), chunk)
            return 0

        lax.fori_loop(1, cached // chunk, step, 0)

    same = lax.broadcasted_iota(jnp.int32, (rows, rows), 0) == lax.broadcasted_iota(
        jnp.int32, (rows, rows), 1
    )

    line = lax.broadcasted_iota(jnp.int32, (16, rows), 0)

    def pack(where, numer, total):
        high = total.astype(bf16).astype(f32)
        low = total - high
        where[0:rows, :] = numer.astype(bf16)
        high, low = jnp.broadcast_to(high, (16, rows)), jnp.broadcast_to(low, (16, rows))
        where[rows:, :] = jnp.where(line == 0, high, jnp.where(line == 1, low, 0.0)).astype(bf16)

    def attend_new(g):
        acc[g] += attend(g, cached, rows)
        for m in range(group):
            i = g * group + m
            block = acc[g, m * rows : (m + 1) * rows, :]
            total = jnp.sum(jnp.where(same, block[:, head:], 0.0), axis=0, keepdims=True)
            if i == own:
                pack(nrecv.at[own], block[:, :head], total)
            else:
                pack(nsend.at[i], block[:, :head], total)
                j = row_inv[i]
                send(nsend.at[i], nrecv.at[j], s_n.at[i], r_n.at[j], row_peer(*row_rel[i]))

    attend_cached(0)
    grad_terms()
    attend_cached(1)
    attend_cached(2)
    grad_send()
    attend_cached(3)
    for i in range(1, n):
        src = (y + i) % n
        arrived(kvpart.at[src], s_kv.at[0], r_kv.at[src])
    fresh = kvpart[0].astype(f32)
    for i in range(1, n):
        fresh = fresh + kvpart[i].astype(f32)
    fresh = fresh.astype(bf16)
    keys[cached:, :] = norm_rows(fresh[:, :head], kgain)
    vals[cached:, 0:head] = fresh[:, head:]
    for g in range(4):
        attend_new(g)

    for j in others:
        arrived(nrecv.at[j], s_n.at[j], r_n.at[j])
    summed = nrecv[own].astype(f32)
    for j in others:
        summed = summed + nrecv[j].astype(f32)
    total = summed[rows : rows + 1, :] + summed[rows + 1 : rows + 2, :]
    att[0, place(0, 0)] = (jnp.transpose(summed[0:rows, :]) / total).astype(bf16)

    gather_start(att, s_a, r_a)
    gather_other(att, s_a, r_a)
    grad = gsum[xh * n + z].astype(f32)
    for j in range(1, 2 * n):
        arrived(grecv.at[j], s_gr.at[j], r_gr.at[j])
        grad = grad + grecv[j].astype(f32)
    grad_out[...] = grad.astype(bf16)
    branch = jnp.zeros((dcols, rows), f32)
    for step in range(n + lag):
        if step < n:
            gather_z(att, s_a, r_a, turns[step])
        if step >= lag:
            i = turns[step - lag]
            gather_core(att, s_a, r_a, i)
            for a in (0, 1):
                right = att[i, 2 * a : 2 * a + 2].reshape(2 * head, rows)
                left = wout[a * n + (z + order[i]) % n]
                branch = branch + jnp.dot(left, right, preferred_element_type=f32)
    gate = jnp.transpose(jnp.broadcast_to(out_gate[...], (rows, dcols)))
    layer_out[...] = (tokv[...].astype(f32) + gate * branch).astype(bf16)

    @pl.when(off_diagonal)
    def _():
        transpose.wait_send()

    for copy in sends:
        copy.wait_send()


def body(n, *args):
    tokens, w_query, w_key, w_value, w_out, key_cache, value_cache, query_gain, key_gain, out_gate, cotangent = args
    rows, dcols = tokens.shape
    flipped = (w_out.shape[1], w_out.shape[0])
    head = query_gain.shape[0]
    kin = w_query.shape[0]
    cached = key_cache.shape[0]
    group = max(n // 2, 1)
    vmem = pl.BlockSpec(memory_space=pltpu.VMEM)
    hbm = pl.BlockSpec(memory_space=pl.ANY)
    dma = pltpu.SemaphoreType.DMA
    scratch = [
        pltpu.VMEM((n, 4, dcols, rows), bf16),
        pltpu.VMEM((2, kin, 3 * head), bf16),
        pltpu.VMEM((2 * n,) + flipped, bf16),
        pltpu.VMEM((cached + rows, head), bf16),
        pltpu.VMEM((cached + rows, 2 * head), bf16),
        pltpu.VMEM((rows, dcols), bf16),
        pltpu.VMEM((n, rows, head), bf16),
        pltpu.VMEM((n, rows, head), bf16),
        pltpu.VMEM((n, rows, 2 * head), bf16),
        pltpu.VMEM((n, rows, 2 * head), bf16),
        pltpu.VMEM((2 * n, rows, head), bf16),
        pltpu.VMEM((2 * n // group, group * rows, 2 * head), f32),
        pltpu.VMEM((2 * n, rows + 16, head), bf16),
        pltpu.VMEM((2 * n, rows + 16, head), bf16),
        pltpu.VMEM((2, 2 * n, rows, head), bf16),
        pltpu.VMEM((2 * n, rows, head), bf16),
        pltpu.VMEM((2 * n, rows, head), bf16),
        pltpu.VMEM((2 * n, rows, head), bf16),
        pltpu.VMEM((n, 4, head, rows), bf16),
        pltpu.VMEM((cached, head), bf16),
        pltpu.VMEM((dcols, rows), bf16),
        pltpu.VMEM((dcols, rows), bf16),
        dma((8,)),
        dma,
        dma,
        dma((3,)),
        dma((3,)),
        dma((n,)),
        dma((n,)),
        dma((n,)),
        dma((n,)),
        dma((4, n)),
        dma((4, n)),
        dma((n,)),
        dma((n,)),
        dma((n,)),
        dma((n,)),
        dma((2 * n,)),
        dma((2 * n,)),
        dma((2 * n,)),
        dma((2 * n,)),
        dma,
        dma,
        dma((2 * n,)),
        dma((2 * n,)),
        dma((4, n)),
        dma((4, n)),
    ]
    layer_out, grad = pl.pallas_call(
        functools.partial(kernel, n),
        name="attention_block",
        out_shape=(
            jax.ShapeDtypeStruct((dcols, rows), bf16),
            jax.ShapeDtypeStruct((rows, head), bf16),
        ),
        in_specs=[hbm] * 7 + [vmem] * 3 + [hbm],
        out_specs=(vmem, vmem),
        scratch_shapes=scratch,
        compiler_params=pltpu.CompilerParams(
            collective_id=0, has_side_effects=True, vmem_limit_bytes=60 * 1024 * 1024
        ),
    )(
        tokens.T,
        w_query,
        w_key,
        w_value,
        w_out.T,
        key_cache,
        value_cache,
        query_gain.reshape(1, head),
        key_gain.reshape(1, head),
        out_gate.reshape(1, dcols),
        cotangent.T,
    )
    return layer_out.T, grad


def solution(mesh):
    n = mesh.shape["row"] // 2
    both = P("row", "col")
    placed = (both,) * 7 + (P(), P(), P("col"), both)
    return jax.shard_map(
        functools.partial(body, n),
        mesh=mesh,
        in_specs=placed,
        out_specs=(both, both),
        check_vma=False,
    )
```

```python
import functools
import math

import jax
import jax.numpy as jnp
from jax import lax
from jax.experimental import pallas as pl
from jax.experimental.pallas import tpu as pltpu
from jax.sharding import PartitionSpec as P

MESH = pl.DeviceIdType.MESH
epsilon = 1e-06
f32 = jnp.float32
bf16 = jnp.bfloat16
FIRST = (((0,), (0,)), ((), ()))
LAST = (((1,), (1,)), ((), ()))


def norm_rows(values, gain):
    wide = values.astype(f32)
    mean_square = jnp.mean(wide * wide, axis=-1, keepdims=True)
    return (wide * lax.rsqrt(mean_square + epsilon) * gain).astype(bf16)


def ring_order(n):
    order = [0]
    for d in range(1, n // 2 + 1):
        order.append(d)
        if (n - d) % n != d:
            order.append(n - d)
    return order


def kernel(
    n,
    tokens,
    w_query,
    w_key,
    w_value,
    w_out,
    key_cache,
    value_cache,
    query_gain,
    key_gain,
    out_gate,
    cotangent,
    layer_out,
    grad_out,
    tok,
    wall,
    wout,
    keys,
    vals,
    scaled,
    qsend,
    qpart,
    kvsend,
    kvpart,
    queries,
    acc,
    nsend,
    nrecv,
    nside,
    gsend,
    gpair,
    gsum,
    grecv,
    att,
    kraw,
    tokv,
    cotv,
    s_in,
    s_t,
    r_t,
    s_w,
    r_w,
    s_wo,
    r_wo,
    s_wx,
    r_wx,
    s_g,
    r_g,
    s_q,
    r_q,
    s_kv,
    r_kv,
    s_qa,
    r_qa,
    s_n,
    r_n,
    r_nx,
    s_gp,
    r_gp,
    s_gr,
    r_gr,
    s_a,
    r_a,
):
    dcols, rows = tokens.shape
    head = query_gain.shape[1]
    cached = key_cache.shape[0]
    row = lax.axis_index("row")
    col = lax.axis_index("col")
    xl, y = row // n, row % n
    xh, z, k = col // (2 * n), (col // 2) % n, col % 2

    def dev(xl_, y_, xh_, z_, k_):
        return (xl_ * n + y_, (xh_ * n + z_) * 2 + k_)

    order = ring_order(n)
    slot_of = {d: i for i, d in enumerate(order)}

    group = max(n // 2, 1)
    near, far = order[:group], order[group:]
    row_rel = [(0, b) for b in near + far] + [(1, b) for b in near + far]
    row_inv = [row_rel.index((a, (n - b) % n)) for a, b in row_rel]
    own = row_rel.index((0, 0))
    others = [i for i in range(2 * n) if i != own]
    if n == 8:
        hops = {0: ((2, None), (6, None), (1, None), (7, None))}
        hops[2] = ((7, None), (6, 0))
        hops[6] = ((1, None), (2, 1))
        turns = [slot_of[d] for d in (2, 6, 0, 1, 7, 3, 5, 4)]
    else:
        hops = {0: tuple((d, None) for d in range(1, n))}
        turns = list(range(n))
    chip_rel = [(a, b) for b in order for a in (0, 1)]
    chip_inv = [chip_rel.index((a, (n - b) % n)) for a, b in chip_rel]
    col_rel = [
        (a, b, c)
        for b in order
        for a in (0, 1)
        for c in (0, 1)
        if (a, b, c) != (0, 0, 0)
    ]

    def row_peer(a, b):
        return dev((xl + a) % 2, (y + b) % n, xh, z, k)

    def col_peer(a, b, c):
        return dev(xl, y, (xh + a) % 2, (z + b) % n, (k + c) % 2)

    def remote(src, dst, ssem, rsem, to):
        return pltpu.make_async_remote_copy(
            src_ref=src, dst_ref=dst, send_sem=ssem, recv_sem=rsem, device_id=to, device_id_type=MESH
        )

    any_peer = col_peer(0, 0, 1)

    def arrived(dst, ssem, rsem):
        remote(dst, dst, ssem, rsem, any_peer).wait_recv()

    sends = []

    def send(src, dst, ssem, rsem, to):
        copy = remote(src, dst, ssem, rsem, to)
        copy.start()
        sends.append(copy)

    barrier = pltpu.get_barrier_semaphore()
    off_diagonal = y != z
    twin = dev(xl, z, xh, y, k)

    @pl.when(off_diagonal)
    def _():
        pl.semaphore_signal(barrier, inc=1, device_id=twin, device_id_type=MESH)

    for i in others:
        pl.semaphore_signal(barrier, inc=1, device_id=row_peer(*row_rel[i]), device_id_type=MESH)
    for rel in col_rel:
        pl.semaphore_signal(barrier, inc=1, device_id=col_peer(*rel), device_id_type=MESH)

    local = [
        (key_cache, kraw),
        (cotangent, cotv),
        (value_cache, vals.at[pl.ds(0, cached), pl.ds(0, head)]),
        (w_query, wall.at[xl, :, pl.ds(0, head)]),
        (w_key, wall.at[xl, :, pl.ds(head, head)]),
        (w_value, wall.at[xl, :, pl.ds(2 * head, head)]),
        (w_out, wout.at[row]),
        (tokens, tokv),
    ]
    loads = [pltpu.make_async_copy(src, dst, s_in.at[i]) for i, (src, dst) in enumerate(local)]
    for load in loads:
        load.start()
    vals[:, head:] = jnp.ones((vals.shape[0], vals.shape[1] - head), bf16)
    kgain = key_gain[...]
    gate = jnp.transpose(jnp.broadcast_to(out_gate[...], (rows, dcols)))
    loads[0].wait()
    keys[0:cached, :] = norm_rows(kraw[...], kgain)
    loads[1].wait()
    scaled[...] = jnp.transpose((cotv[...].astype(f32) * gate).astype(bf16))
    for load in loads[2:]:
        load.wait()

    peers = len(row_rel) - 1 + len(col_rel)

    @pl.when(off_diagonal)
    def _():
        pl.semaphore_wait(barrier, peers + 1)

    @pl.when(jnp.logical_not(off_diagonal))
    def _():
        pl.semaphore_wait(barrier, peers)

    first = tok.at[0, 2 * xh + k]
    transpose = remote(tokens, first, s_t, r_t, twin)
    stay = pltpu.make_async_copy(tokens, first, r_t)

    @pl.when(off_diagonal)
    def _():
        transpose.start()

    @pl.when(jnp.logical_not(off_diagonal))
    def _():
        stay.start()

    x_near = row_peer(1, 0)
    for i, w in enumerate((w_query, w_key, w_value)):
        send(w, wall.at[xl, :, pl.ds(i * head, head)], s_w.at[i], r_w.at[i], x_near)


    def pass_weights(*slots):
        for i in slots:
            if i < n:
                block = wout.at[xl * n + (y + order[i]) % n]
                arrived(block, s_wo.at[i], r_wo.at[i])
                for step, only in hops.get(order[i], ()):
                    if not only:
                        j = slot_of[(order[i] - step) % n]
                        send(block, block, s_wo.at[j], r_wo.at[j], row_peer(0, step))
                send(block, block, s_wx.at[i], r_wx.at[i], x_near)

    @pl.when(off_diagonal)
    def _():
        transpose.wait_recv()

    @pl.when(jnp.logical_not(off_diagonal))
    def _():
        stay.wait()

    def place(a, c):
        return ((xh + a) % 2) * 2 + (k + c) % 2

    def relay(buf, ss, rs, a, d):
        block = buf.at[slot_of[d], place(a, 0)]
        for step, only in hops.get(d, ()):
            if only is None or only == a:
                j = slot_of[(d - step) % n]
                send(block, buf.at[j, place(a, 0)], ss.at[a, j], rs.at[a, j], col_peer(0, step, 0))

    def share(buf, ss, rs, a, i):
        block = buf.at[i, place(a, 0)]
        send(block, block, ss.at[2 + a, i], rs.at[2 + a, i], col_peer(0, 0, 1))

    def gather_start(buf, ss, rs):
        block = buf.at[0, place(0, 0)]
        for step, _ in hops[0][:2]:
            j = slot_of[(n - step) % n]
            for a in (0, 1):
                send(block, buf.at[j, place(0, 0)], ss.at[a, j], rs.at[a, j], col_peer(a, step, 0))
        send(block, block, ss.at[1, 0], rs.at[1, 0], col_peer(1, 0, 0))
        for step, _ in hops[0][2:]:
            j = slot_of[(n - step) % n]
            for a in (0, 1):
                send(block, buf.at[j, place(0, 0)], ss.at[a, j], rs.at[a, j], col_peer(a, step, 0))
        share(buf, ss, rs, 0, 0)

    def gather_z(buf, ss, rs, i):
        for a in (0, 1):
            if i or a:
                arrived(buf.at[i, place(a, 0)], ss.at[a, i], rs.at[a, i])
                if i:
                    relay(buf, ss, rs, a, order[i])
                share(buf, ss, rs, a, i)

    def gather_core(buf, ss, rs, i):
        for a in (0, 1):
            arrived(buf.at[i, place(a, 1)], ss.at[2 + a, i], rs.at[2 + a, i])

    lag = 2

    def project(slot, lo, width):
        left = tok[slot].reshape(4 * dcols, rows)
        right = wall[:, :, lo : lo + width].reshape(4 * dcols, width)
        return lax.dot_general(left, right, FIRST, preferred_element_type=f32).astype(bf16)

    gather_start(tok, s_g, r_g)
    for step, _ in hops[0]:
        j = slot_of[(n - step) % n]
        send(w_out, wout.at[row], s_wo.at[j], r_wo.at[j], row_peer(0, step))
    send(w_out, wout.at[row], s_wx.at[0], r_wx.at[0], x_near)
    weights_here = False
    for step in range(n + lag):
        if step < n:
            gather_z(tok, s_g, r_g, turns[step])
        if step == 2:
            pass_weights(3, 4)
        if step >= lag:
            i = turns[step - lag]
            gather_core(tok, s_g, r_g, i)
            if not weights_here:
                weights_here = True
                for j in range(3):
                    part = wall.at[1 - xl, :, pl.ds(j * head, head)]
                    arrived(part, s_w.at[j], r_w.at[j])
            value = project(i, 0, 3 * head)
            owner = (z + order[i]) % n
            qsend[owner] = value[:, :head]
            kvsend[owner] = value[:, head:]
    for d in reversed(order[1:]):
        owner = (y + d) % n
        send(qsend.at[owner], qpart.at[y], s_q.at[d], r_q.at[y], row_peer(0, d))
    qpart[y] = qsend[y]
    kvpart[y] = kvsend[y]
    pass_weights(1, 2, *range(5, n))

    for i in range(1, n):
        src = (y + i) % n
        arrived(qpart.at[src], s_q.at[0], r_q.at[src])
    query = qpart[0].astype(f32)
    for i in range(1, n):
        query = query + qpart[i].astype(f32)
    queries[own] = norm_rows(query.astype(bf16), query_gain[...])
    send(queries.at[own], queries.at[n], s_qa.at[n], r_qa.at[n], x_near)
    for d in order[1:]:
        i = slot_of[d]
        j = slot_of[n - d]
        send(queries.at[own], queries.at[j], s_qa.at[i], r_qa.at[j], row_peer(0, d))
    for d in reversed(order[1:]):
        owner = (y + d) % n
        send(kvsend.at[owner], kvpart.at[y], s_kv.at[d], r_kv.at[y], row_peer(0, d))

    def grad_block(j, _):
        terms = jnp.dot(scaled[...], wout[j], preferred_element_type=f32)
        for c in (0, 1):
            gsend[c, j] = terms[:, c * head : (c + 1) * head].astype(bf16)
        return 0

    def grad_terms():
        for i in range(n):
            src = (y + order[i]) % n
            arrived(wout.at[(1 - xl) * n + src], s_wx.at[i], r_wx.at[i])

        lax.fori_loop(0, 2 * n, grad_block, 0)
        send(gsend.at[1 - k], gpair, s_gp, r_gp, col_peer(0, 0, 1))

    def grad_send():
        arrived(gpair, s_gp, r_gp)
        gsum[...] = (gsend[k].astype(f32) + gpair[...].astype(f32)).astype(bf16)
        for i, (a, b) in enumerate(chip_rel):
            if i:
                chip = ((xh + a) % 2) * n + (z + b) % n
                j = chip_inv[i]
                send(gsum.at[chip], grecv.at[j], s_gr.at[i], r_gr.at[j], col_peer(a, b, 0))

    factor = math.log2(math.e) * head ** (-0.5)
    n_groups = 2 * n // group
    lines = group * rows
    chunk = min(512, cached)

    def attend(g, lo, size):
        query = queries[g * group : (g + 1) * group].reshape(lines, head)
        scores = lax.dot_general(query, keys[pl.ds(lo, size), :], LAST, preferred_element_type=f32)
        weights = jnp.exp2(scores * factor).astype(bf16)
        return jnp.dot(weights, vals[pl.ds(lo, size), :], preferred_element_type=f32)

    def attend_cached(g):
        for i in range(g * group, (g + 1) * group):
            if i == own:
                continue
            arrived(queries.at[i], s_qa.at[i], r_qa.at[i])
            if i < n:
                send(queries.at[i], queries.at[n + i], s_qa.at[n + i], r_qa.at[n + i], x_near)
        acc[g] = attend(g, 0, chunk)

        def step(i, _):
            acc[g] += attend(g, pl.multiple_of(i * chunk, chunk), chunk)
            return 0

        lax.fori_loop(1, cached // chunk, step, 0)

    same = lax.broadcasted_iota(jnp.int32, (rows, rows), 0) == lax.broadcasted_iota(
        jnp.int32, (rows, rows), 1
    )

    line = lax.broadcasted_iota(jnp.int32, (16, rows), 0)

    def pack(where, numer, total):
        high = total.astype(bf16).astype(f32)
        low = total - high
        where[0:rows, :] = numer.astype(bf16)
        high, low = jnp.broadcast_to(high, (16, rows)), jnp.broadcast_to(low, (16, rows))
        where[rows:, :] = jnp.where(line == 0, high, jnp.where(line == 1, low, 0.0)).astype(bf16)

    def attend_new(g):
        acc[g] += attend(g, cached, rows)
        for m in range(group):
            i = g * group + m
            a, b = row_rel[i]
            t = slot_of[b]
            block = acc[g, m * rows : (m + 1) * rows, :]
            numer = block[:, :head]
            total = jnp.sum(jnp.where(same, block[:, head:], 0.0), axis=0, keepdims=True)
            if a:
                pack(nsend.at[i], numer, total)
                send(nsend.at[i], nside.at[t], s_n.at[i], r_nx.at[t], x_near)
                continue
            arrived(nside.at[t], s_n.at[i], r_nx.at[t])
            side = nside[t].astype(f32)
            numer = numer + side[0:rows, :]
            total = total + side[rows : rows + 1, :] + side[rows + 1 : rows + 2, :]
            if i == own:
                pack(nrecv.at[own], numer, total)
            else:
                pack(nsend.at[i], numer, total)
                j = row_inv[i]
                send(nsend.at[i], nrecv.at[j], s_n.at[i], r_n.at[j], row_peer(0, b))

    grad_terms()
    attend_cached(0)
    grad_send()
    attend_cached(1)
    attend_cached(2)
    attend_cached(3)
    for i in range(1, n):
        src = (y + i) % n
        arrived(kvpart.at[src], s_kv.at[0], r_kv.at[src])
    fresh = kvpart[0].astype(f32)
    for i in range(1, n):
        fresh = fresh + kvpart[i].astype(f32)
    fresh = fresh.astype(bf16)
    keys[cached:, :] = norm_rows(fresh[:, :head], kgain)
    vals[cached:, 0:head] = fresh[:, head:]
    for g in (3, 2, 1, 0):
        attend_new(g)

    for j in range(1, n):
        arrived(nrecv.at[j], s_n.at[j], r_n.at[j])
    summed = nrecv[own].astype(f32)
    for j in range(1, n):
        summed = summed + nrecv[j].astype(f32)
    total = summed[rows : rows + 1, :] + summed[rows + 1 : rows + 2, :]
    att[0, place(0, 0)] = (jnp.transpose(summed[0:rows, :]) / total).astype(bf16)

    gather_start(att, s_a, r_a)
    grad = gsum[xh * n + z].astype(f32)
    for j in range(1, 2 * n):
        arrived(grecv.at[j], s_gr.at[j], r_gr.at[j])
        grad = grad + grecv[j].astype(f32)
    grad_out[...] = grad.astype(bf16)
    branch = jnp.zeros((dcols, rows), f32)
    for step in range(n + lag):
        if step < n:
            gather_z(att, s_a, r_a, turns[step])
        if step >= lag:
            i = turns[step - lag]
            gather_core(att, s_a, r_a, i)
            for a in (0, 1):
                right = att[i, 2 * a : 2 * a + 2].reshape(2 * head, rows)
                left = wout[a * n + (z + order[i]) % n]
                branch = branch + jnp.dot(left, right, preferred_element_type=f32)
    gate = jnp.transpose(jnp.broadcast_to(out_gate[...], (rows, dcols)))
    layer_out[...] = (tokv[...].astype(f32) + gate * branch).astype(bf16)

    @pl.when(off_diagonal)
    def _():
        transpose.wait_send()

    for copy in sends:
        copy.wait_send()


def body(n, *args):
    tokens, w_query, w_key, w_value, w_out, key_cache, value_cache, query_gain, key_gain, out_gate, cotangent = args
    rows, dcols = tokens.shape
    flipped = (w_out.shape[1], w_out.shape[0])
    head = query_gain.shape[0]
    kin = w_query.shape[0]
    cached = key_cache.shape[0]
    group = max(n // 2, 1)
    vmem = pl.BlockSpec(memory_space=pltpu.VMEM)
    hbm = pl.BlockSpec(memory_space=pl.ANY)
    dma = pltpu.SemaphoreType.DMA
    scratch = [
        pltpu.VMEM((n, 4, dcols, rows), bf16),
        pltpu.VMEM((2, kin, 3 * head), bf16),
        pltpu.VMEM((2 * n,) + flipped, bf16),
        pltpu.VMEM((cached + rows, head), bf16),
        pltpu.VMEM((cached + rows, 2 * head), bf16),
        pltpu.VMEM((rows, dcols), bf16),
        pltpu.VMEM((n, rows, head), bf16),
        pltpu.VMEM((n, rows, head), bf16),
        pltpu.VMEM((n, rows, 2 * head), bf16),
        pltpu.VMEM((n, rows, 2 * head), bf16),
        pltpu.VMEM((2 * n, rows, head), bf16),
        pltpu.VMEM((2 * n // group, group * rows, 2 * head), f32),
        pltpu.VMEM((2 * n, rows + 16, head), bf16),
        pltpu.VMEM((n, rows + 16, head), bf16),
        pltpu.VMEM((n, rows + 16, head), bf16),
        pltpu.VMEM((2, 2 * n, rows, head), bf16),
        pltpu.VMEM((2 * n, rows, head), bf16),
        pltpu.VMEM((2 * n, rows, head), bf16),
        pltpu.VMEM((2 * n, rows, head), bf16),
        pltpu.VMEM((n, 4, head, rows), bf16),
        pltpu.VMEM((cached, head), bf16),
        pltpu.VMEM((dcols, rows), bf16),
        pltpu.VMEM((dcols, rows), bf16),
        dma((8,)),
        dma,
        dma,
        dma((3,)),
        dma((3,)),
        dma((n,)),
        dma((n,)),
        dma((n,)),
        dma((n,)),
        dma((4, n)),
        dma((4, n)),
        dma((n,)),
        dma((n,)),
        dma((n,)),
        dma((n,)),
        dma((2 * n,)),
        dma((2 * n,)),
        dma((2 * n,)),
        dma((n,)),
        dma((n,)),
        dma,
        dma,
        dma((2 * n,)),
        dma((2 * n,)),
        dma((4, n)),
        dma((4, n)),
    ]
    layer_out, grad = pl.pallas_call(
        functools.partial(kernel, n),
        name="attention_block",
        out_shape=(
            jax.ShapeDtypeStruct((dcols, rows), bf16),
            jax.ShapeDtypeStruct((rows, head), bf16),
        ),
        in_specs=[hbm] * 7 + [vmem] * 3 + [hbm],
        out_specs=(vmem, vmem),
        scratch_shapes=scratch,
        compiler_params=pltpu.CompilerParams(
            collective_id=0, has_side_effects=True, vmem_limit_bytes=60 * 1024 * 1024
        ),
    )(
        tokens.T,
        w_query,
        w_key,
        w_value,
        w_out.T,
        key_cache,
        value_cache,
        query_gain.reshape(1, head),
        key_gain.reshape(1, head),
        out_gate.reshape(1, dcols),
        cotangent.T,
    )
    return layer_out.T, grad


def solution(mesh):
    n = mesh.shape["row"] // 2
    both = P("row", "col")
    placed = (both,) * 7 + (P(), P(), P("col"), both)
    return jax.shard_map(
        functools.partial(body, n),
        mesh=mesh,
        in_specs=placed,
        out_specs=(both, both),
        check_vma=False,
    )
```

```python
import functools
import math

import jax
import jax.numpy as jnp
from jax import lax
from jax.experimental import pallas as pl
from jax.experimental.pallas import tpu as pltpu
from jax.sharding import PartitionSpec as P

MESH = pl.DeviceIdType.MESH
epsilon = 1e-06
f32 = jnp.float32
bf16 = jnp.bfloat16
FIRST = (((0,), (0,)), ((), ()))
LAST = (((1,), (1,)), ((), ()))


def norm_rows(values, gain):
    wide = values.astype(f32)
    mean_square = jnp.mean(wide * wide, axis=-1, keepdims=True)
    return (wide * lax.rsqrt(mean_square + epsilon) * gain).astype(bf16)


def ring_order(n):
    order = [0]
    for d in range(1, n // 2 + 1):
        order.append(d)
        if (n - d) % n != d:
            order.append(n - d)
    return order


def kernel(
    n,
    tokens,
    w_query,
    w_key,
    w_value,
    w_out,
    key_cache,
    value_cache,
    query_gain,
    key_gain,
    out_gate,
    cotangent,
    layer_out,
    grad_out,
    tok,
    wall,
    wout,
    keys,
    vals,
    scaled,
    qsend,
    qpart,
    kvsend,
    kvpart,
    queries,
    acc,
    nsend,
    nrecv,
    nside,
    gsend,
    gpair,
    gsum,
    grecv,
    att,
    kraw,
    tokv,
    cotv,
    s_in,
    s_t,
    r_t,
    s_w,
    r_w,
    s_wo,
    r_wo,
    s_wx,
    r_wx,
    s_g,
    r_g,
    s_q,
    r_q,
    s_kv,
    r_kv,
    s_qa,
    r_qa,
    s_n,
    r_n,
    r_nx,
    s_gp,
    r_gp,
    s_gr,
    r_gr,
    s_a,
    r_a,
):
    dcols, rows = tokens.shape
    head = query_gain.shape[1]
    cached = key_cache.shape[0]
    row = lax.axis_index("row")
    col = lax.axis_index("col")
    xl, y = row // n, row % n
    xh, z, k = col // (2 * n), (col // 2) % n, col % 2

    def dev(xl_, y_, xh_, z_, k_):
        return (xl_ * n + y_, (xh_ * n + z_) * 2 + k_)

    order = ring_order(n)
    slot_of = {d: i for i, d in enumerate(order)}

    group = max(n // 2, 1)
    near, far = order[:group], order[group:]
    row_rel = [(0, b) for b in near + far] + [(1, b) for b in near + far]
    row_inv = [row_rel.index((a, (n - b) % n)) for a, b in row_rel]
    own = row_rel.index((0, 0))
    others = [i for i in range(2 * n) if i != own]
    if n == 8:
        hops = {0: ((2, None), (6, None), (1, None), (7, None))}
        hops[2] = ((7, None), (6, 0))
        hops[6] = ((1, None), (2, 1))
        turns = [slot_of[d] for d in (2, 6, 0, 1, 7, 3, 5, 4)]
    else:
        hops = {0: tuple((d, None) for d in range(1, n))}
        turns = list(range(n))
    chip_rel = [(a, b) for b in order for a in (0, 1)]
    chip_inv = [chip_rel.index((a, (n - b) % n)) for a, b in chip_rel]
    col_rel = [
        (a, b, c)
        for b in order
        for a in (0, 1)
        for c in (0, 1)
        if (a, b, c) != (0, 0, 0)
    ]

    def row_peer(a, b):
        return dev((xl + a) % 2, (y + b) % n, xh, z, k)

    def col_peer(a, b, c):
        return dev(xl, y, (xh + a) % 2, (z + b) % n, (k + c) % 2)

    def remote(src, dst, ssem, rsem, to):
        return pltpu.make_async_remote_copy(
            src_ref=src, dst_ref=dst, send_sem=ssem, recv_sem=rsem, device_id=to, device_id_type=MESH
        )

    any_peer = col_peer(0, 0, 1)

    def arrived(dst, ssem, rsem):
        remote(dst, dst, ssem, rsem, any_peer).wait_recv()

    sends = []

    def send(src, dst, ssem, rsem, to):
        copy = remote(src, dst, ssem, rsem, to)
        copy.start()
        sends.append(copy)

    barrier = pltpu.get_barrier_semaphore()
    off_diagonal = y != z
    twin = dev(xl, z, xh, y, k)

    @pl.when(off_diagonal)
    def _():
        pl.semaphore_signal(barrier, inc=1, device_id=twin, device_id_type=MESH)

    for i in others:
        pl.semaphore_signal(barrier, inc=1, device_id=row_peer(*row_rel[i]), device_id_type=MESH)
    for rel in col_rel:
        pl.semaphore_signal(barrier, inc=1, device_id=col_peer(*rel), device_id_type=MESH)

    local = [
        (key_cache, kraw),
        (cotangent, cotv),
        (value_cache, vals.at[pl.ds(0, cached), pl.ds(0, head)]),
        (w_query, wall.at[xl, :, pl.ds(0, head)]),
        (w_key, wall.at[xl, :, pl.ds(head, head)]),
        (w_value, wall.at[xl, :, pl.ds(2 * head, head)]),
        (w_out, wout.at[row]),
        (tokens, tokv),
    ]
    loads = [pltpu.make_async_copy(src, dst, s_in.at[i]) for i, (src, dst) in enumerate(local)]
    for load in loads:
        load.start()
    vals[:, head:] = jnp.ones((vals.shape[0], vals.shape[1] - head), bf16)
    kgain = key_gain[...]
    gate = jnp.transpose(jnp.broadcast_to(out_gate[...], (rows, dcols)))
    loads[0].wait()
    keys[0:cached, :] = norm_rows(kraw[...], kgain)
    loads[1].wait()
    scaled[...] = jnp.transpose((cotv[...].astype(f32) * gate).astype(bf16))
    for load in loads[2:]:
        load.wait()

    peers = len(row_rel) - 1 + len(col_rel)

    @pl.when(off_diagonal)
    def _():
        pl.semaphore_wait(barrier, peers + 1)

    @pl.when(jnp.logical_not(off_diagonal))
    def _():
        pl.semaphore_wait(barrier, peers)

    first = tok.at[0, 2 * xh + k]
    transpose = remote(tokens, first, s_t, r_t, twin)
    stay = pltpu.make_async_copy(tokens, first, r_t)

    @pl.when(off_diagonal)
    def _():
        transpose.start()

    @pl.when(jnp.logical_not(off_diagonal))
    def _():
        stay.start()

    x_near = row_peer(1, 0)
    for i, w in enumerate((w_query, w_key, w_value)):
        send(w, wall.at[xl, :, pl.ds(i * head, head)], s_w.at[i], r_w.at[i], x_near)


    def pass_weights(*slots):
        for i in slots:
            if i < n:
                block = wout.at[xl * n + (y + order[i]) % n]
                arrived(block, s_wo.at[i], r_wo.at[i])
                for step, only in hops.get(order[i], ()):
                    if not only:
                        j = slot_of[(order[i] - step) % n]
                        send(block, block, s_wo.at[j], r_wo.at[j], row_peer(0, step))
                send(block, block, s_wx.at[i], r_wx.at[i], x_near)

    @pl.when(off_diagonal)
    def _():
        transpose.wait_recv()

    @pl.when(jnp.logical_not(off_diagonal))
    def _():
        stay.wait()

    def place(a, c):
        return ((xh + a) % 2) * 2 + (k + c) % 2

    def relay(buf, ss, rs, a, d):
        block = buf.at[slot_of[d], place(a, 0)]
        for step, only in hops.get(d, ()):
            if only is None or only == a:
                j = slot_of[(d - step) % n]
                send(block, buf.at[j, place(a, 0)], ss.at[a, j], rs.at[a, j], col_peer(0, step, 0))

    def share(buf, ss, rs, a, i):
        block = buf.at[i, place(a, 0)]
        send(block, block, ss.at[2 + a, i], rs.at[2 + a, i], col_peer(0, 0, 1))

    def gather_start(buf, ss, rs):
        block = buf.at[0, place(0, 0)]
        for step, _ in hops[0][:2]:
            j = slot_of[(n - step) % n]
            for a in (0, 1):
                send(block, buf.at[j, place(0, 0)], ss.at[a, j], rs.at[a, j], col_peer(a, step, 0))
        send(block, block, ss.at[1, 0], rs.at[1, 0], col_peer(1, 0, 0))
        for step, _ in hops[0][2:]:
            j = slot_of[(n - step) % n]
            for a in (0, 1):
                send(block, buf.at[j, place(0, 0)], ss.at[a, j], rs.at[a, j], col_peer(a, step, 0))
        share(buf, ss, rs, 0, 0)

    def gather_z(buf, ss, rs, i):
        for a in (0, 1):
            if i or a:
                arrived(buf.at[i, place(a, 0)], ss.at[a, i], rs.at[a, i])
                if i:
                    relay(buf, ss, rs, a, order[i])
                share(buf, ss, rs, a, i)

    def gather_core(buf, ss, rs, i):
        for a in (0, 1):
            arrived(buf.at[i, place(a, 1)], ss.at[2 + a, i], rs.at[2 + a, i])

    lag = 2

    def project(slot, lo, width):
        left = tok[slot].reshape(4 * dcols, rows)
        right = wall[:, :, lo : lo + width].reshape(4 * dcols, width)
        return lax.dot_general(left, right, FIRST, preferred_element_type=f32).astype(bf16)

    gather_start(tok, s_g, r_g)
    for step, _ in hops[0]:
        j = slot_of[(n - step) % n]
        send(w_out, wout.at[row], s_wo.at[j], r_wo.at[j], row_peer(0, step))
    send(w_out, wout.at[row], s_wx.at[0], r_wx.at[0], x_near)
    weights_here = False
    for step in range(n + lag):
        if step < n:
            gather_z(tok, s_g, r_g, turns[step])
        if step == 2:
            pass_weights(3, 4)
        if step == 5:
            pass_weights(1, 2)
        if step >= lag:
            i = turns[step - lag]
            gather_core(tok, s_g, r_g, i)
            if not weights_here:
                weights_here = True
                for j in range(3):
                    part = wall.at[1 - xl, :, pl.ds(j * head, head)]
                    arrived(part, s_w.at[j], r_w.at[j])
            value = project(i, 0, 3 * head)
            owner = (z + order[i]) % n
            qsend[owner] = value[:, :head]
            kvsend[owner] = value[:, head:]
    for d in reversed(order[1:]):
        owner = (y + d) % n
        send(qsend.at[owner], qpart.at[y], s_q.at[d], r_q.at[y], row_peer(0, d))
    qpart[y] = qsend[y]
    kvpart[y] = kvsend[y]
    if n < 5:
        pass_weights(1, 2)
    pass_weights(*range(5, n))

    for i in range(1, n):
        src = (y + i) % n
        arrived(qpart.at[src], s_q.at[0], r_q.at[src])
    query = qpart[0].astype(f32)
    for i in range(1, n):
        query = query + qpart[i].astype(f32)
    factor = math.log2(math.e) * head ** (-0.5)
    queries[own] = norm_rows(query.astype(bf16), query_gain[...] * factor)
    send(queries.at[own], queries.at[n], s_qa.at[n], r_qa.at[n], x_near)
    for d in order[1:]:
        i = slot_of[d]
        j = slot_of[n - d]
        send(queries.at[own], queries.at[j], s_qa.at[i], r_qa.at[j], row_peer(0, d))

    def grad_block(j, _):
        terms = jnp.dot(scaled[...], wout[j], preferred_element_type=f32)
        for c in (0, 1):
            gsend[c, j] = terms[:, c * head : (c + 1) * head].astype(bf16)
        return 0

    def grad_terms():
        for i in range(n):
            src = (y + order[i]) % n
            arrived(wout.at[(1 - xl) * n + src], s_wx.at[i], r_wx.at[i])

        lax.fori_loop(0, 2 * n, grad_block, 0)
        send(gsend.at[1 - k], gpair, s_gp, r_gp, col_peer(0, 0, 1))

    def grad_send():
        arrived(gpair, s_gp, r_gp)
        gsum[...] = (gsend[k].astype(f32) + gpair[...].astype(f32)).astype(bf16)
        for i, (a, b) in enumerate(chip_rel):
            if i:
                chip = ((xh + a) % 2) * n + (z + b) % n
                j = chip_inv[i]
                send(gsum.at[chip], grecv.at[j], s_gr.at[i], r_gr.at[j], col_peer(a, b, 0))

    n_groups = 2 * n // group
    lines = group * rows
    chunk = min(512, cached)

    def attend(g, lo, size):
        query = queries[g * group : (g + 1) * group].reshape(lines, head)
        scores = lax.dot_general(query, keys[pl.ds(lo, size), :], LAST, preferred_element_type=f32)
        weights = jnp.exp2(scores).astype(bf16)
        return jnp.dot(weights, vals[pl.ds(lo, size), :], preferred_element_type=f32)

    def attend_cached(g):
        for i in range(g * group, (g + 1) * group):
            if i == own:
                continue
            arrived(queries.at[i], s_qa.at[i], r_qa.at[i])
            if i < n:
                send(queries.at[i], queries.at[n + i], s_qa.at[n + i], r_qa.at[n + i], x_near)
        acc[g] = attend(g, 0, chunk)

        def step(i, _):
            acc[g] += attend(g, pl.multiple_of(i * chunk, chunk), chunk)
            return 0

        lax.fori_loop(1, cached // chunk, step, 0)

    same = lax.broadcasted_iota(jnp.int32, (rows, rows), 0) == lax.broadcasted_iota(
        jnp.int32, (rows, rows), 1
    )

    line = lax.broadcasted_iota(jnp.int32, (16, rows), 0)

    def pack(where, numer, total):
        high = total.astype(bf16).astype(f32)
        low = total - high
        where[0:rows, :] = numer.astype(bf16)
        high, low = jnp.broadcast_to(high, (16, rows)), jnp.broadcast_to(low, (16, rows))
        where[rows:, :] = jnp.where(line == 0, high, jnp.where(line == 1, low, 0.0)).astype(bf16)

    def attend_new(g):
        acc[g] += attend(g, cached, rows)
        for m in range(group):
            i = g * group + m
            a, b = row_rel[i]
            t = slot_of[b]
            block = acc[g, m * rows : (m + 1) * rows, :]
            numer = block[:, :head]
            total = jnp.sum(jnp.where(same, block[:, head:], 0.0), axis=0, keepdims=True)
            if a:
                pack(nsend.at[i], numer, total)
                send(nsend.at[i], nside.at[t], s_n.at[i], r_nx.at[t], x_near)
                continue
            arrived(nside.at[t], s_n.at[i], r_nx.at[t])
            side = nside[t].astype(f32)
            numer = numer + side[0:rows, :]
            total = total + side[rows : rows + 1, :] + side[rows + 1 : rows + 2, :]
            if i == own:
                pack(nrecv.at[own], numer, total)
            else:
                pack(nsend.at[i], numer, total)
                j = row_inv[i]
                send(nsend.at[i], nrecv.at[j], s_n.at[i], r_n.at[j], row_peer(0, b))

    grad_terms()
    for d in reversed(order[1:]):
        owner = (y + d) % n
        send(kvsend.at[owner], kvpart.at[y], s_kv.at[d], r_kv.at[y], row_peer(0, d))
    attend_cached(0)
    grad_send()
    attend_cached(1)
    attend_cached(2)
    attend_cached(3)
    for i in range(1, n):
        src = (y + i) % n
        arrived(kvpart.at[src], s_kv.at[0], r_kv.at[src])
    fresh = kvpart[0].astype(f32)
    for i in range(1, n):
        fresh = fresh + kvpart[i].astype(f32)
    fresh = fresh.astype(bf16)
    keys[cached:, :] = norm_rows(fresh[:, :head], kgain)
    vals[cached:, 0:head] = fresh[:, head:]
    attend_new(3)
    attend_new(2)
    attend_new(1)
    attend_new(0)

    for j in range(1, n):
        arrived(nrecv.at[j], s_n.at[j], r_n.at[j])
    summed = nrecv[own].astype(f32)
    for j in range(1, n):
        summed = summed + nrecv[j].astype(f32)
    total = summed[rows : rows + 1, :] + summed[rows + 1 : rows + 2, :]
    att[0, place(0, 0)] = (jnp.transpose(summed[0:rows, :]) / total).astype(bf16)

    gather_start(att, s_a, r_a)
    grad = gsum[xh * n + z].astype(f32)
    for j in range(1, 2 * n):
        arrived(grecv.at[j], s_gr.at[j], r_gr.at[j])
        grad = grad + grecv[j].astype(f32)
    grad_out[...] = grad.astype(bf16)
    branch = jnp.zeros((dcols, rows), f32)
    for step in range(n + lag):
        if step < n:
            gather_z(att, s_a, r_a, turns[step])
        if step >= lag:
            i = turns[step - lag]
            gather_core(att, s_a, r_a, i)
            for a in (0, 1):
                right = att[i, 2 * a : 2 * a + 2].reshape(2 * head, rows)
                left = wout[a * n + (z + order[i]) % n]
                branch = branch + jnp.dot(left, right, preferred_element_type=f32)
    gate = jnp.transpose(jnp.broadcast_to(out_gate[...], (rows, dcols)))
    layer_out[...] = (tokv[...].astype(f32) + gate * branch).astype(bf16)

    @pl.when(off_diagonal)
    def _():
        transpose.wait_send()

    for copy in sends:
        copy.wait_send()


def body(n, *args):
    tokens, w_query, w_key, w_value, w_out, key_cache, value_cache, query_gain, key_gain, out_gate, cotangent = args
    rows, dcols = tokens.shape
    flipped = (w_out.shape[1], w_out.shape[0])
    head = query_gain.shape[0]
    kin = w_query.shape[0]
    cached = key_cache.shape[0]
    group = max(n // 2, 1)
    vmem = pl.BlockSpec(memory_space=pltpu.VMEM)
    hbm = pl.BlockSpec(memory_space=pl.ANY)
    dma = pltpu.SemaphoreType.DMA
    scratch = [
        pltpu.VMEM((n, 4, dcols, rows), bf16),
        pltpu.VMEM((2, kin, 3 * head), bf16),
        pltpu.VMEM((2 * n,) + flipped, bf16),
        pltpu.VMEM((cached + rows, head), bf16),
        pltpu.VMEM((cached + rows, 2 * head), bf16),
        pltpu.VMEM((rows, dcols), bf16),
        pltpu.VMEM((n, rows, head), bf16),
        pltpu.VMEM((n, rows, head), bf16),
        pltpu.VMEM((n, rows, 2 * head), bf16),
        pltpu.VMEM((n, rows, 2 * head), bf16),
        pltpu.VMEM((2 * n, rows, head), bf16),
        pltpu.VMEM((2 * n // group, group * rows, 2 * head), f32),
        pltpu.VMEM((2 * n, rows + 16, head), bf16),
        pltpu.VMEM((n, rows + 16, head), bf16),
        pltpu.VMEM((n, rows + 16, head), bf16),
        pltpu.VMEM((2, 2 * n, rows, head), bf16),
        pltpu.VMEM((2 * n, rows, head), bf16),
        pltpu.VMEM((2 * n, rows, head), bf16),
        pltpu.VMEM((2 * n, rows, head), bf16),
        pltpu.VMEM((n, 4, head, rows), bf16),
        pltpu.VMEM((cached, head), bf16),
        pltpu.VMEM((dcols, rows), bf16),
        pltpu.VMEM((dcols, rows), bf16),
        dma((8,)),
        dma,
        dma,
        dma((3,)),
        dma((3,)),
        dma((n,)),
        dma((n,)),
        dma((n,)),
        dma((n,)),
        dma((4, n)),
        dma((4, n)),
        dma((n,)),
        dma((n,)),
        dma((n,)),
        dma((n,)),
        dma((2 * n,)),
        dma((2 * n,)),
        dma((2 * n,)),
        dma((n,)),
        dma((n,)),
        dma,
        dma,
        dma((2 * n,)),
        dma((2 * n,)),
        dma((4, n)),
        dma((4, n)),
    ]
    layer_out, grad = pl.pallas_call(
        functools.partial(kernel, n),
        name="attention_block",
        out_shape=(
            jax.ShapeDtypeStruct((dcols, rows), bf16),
            jax.ShapeDtypeStruct((rows, head), bf16),
        ),
        in_specs=[hbm] * 7 + [vmem] * 3 + [hbm],
        out_specs=(vmem, vmem),
        scratch_shapes=scratch,
        compiler_params=pltpu.CompilerParams(
            collective_id=0, has_side_effects=True, vmem_limit_bytes=60 * 1024 * 1024
        ),
    )(
        tokens.T,
        w_query,
        w_key,
        w_value,
        w_out.T,
        key_cache,
        value_cache,
        query_gain.reshape(1, head),
        key_gain.reshape(1, head),
        out_gate.reshape(1, dcols),
        cotangent.T,
    )
    return layer_out.T, grad


def solution(mesh):
    n = mesh.shape["row"] // 2
    both = P("row", "col")
    placed = (both,) * 7 + (P(), P(), P("col"), both)
    return jax.shard_map(
        functools.partial(body, n),
        mesh=mesh,
        in_specs=placed,
        out_specs=(both, both),
        check_vma=False,
    )
```
